128 devices in a mesh: region: 16 (over y, z_hi, core), pos: 8 (over z_lo, x).
Axes of the slice: x: 4, y: 4, z: 4 (z_hi: 2, z_lo: 2; z = z_hi * 2 + z_lo), core: 2. Of those that a mesh axis runs over, the one named last changes fastest.
Arguments:
- object_tiles: float32 [256, 2, 2, 128, 128], P('region'), may hold values from -4 to 4
- probe: float32 [4, 2, 256, 256], replicated, may hold values from -3 to 3
- fresnel_phase: float32 [256, 256], replicated, may hold values from -3.140625 to 3.140625
- patterns: float32 [16, 8, 2, 256, 256], P('region', 'pos'), may hold values from 0 to 4
- row_offsets: int32 [16, 8, 2], P('region', 'pos'), may hold values from 0 to 3840, as said below
- col_offsets: int32 [16, 8, 2], P('region', 'pos'), may hold values from 0 to 768
- counts: int32 [16, 8], P('region', 'pos'), may hold values from 1 to 2, as said below
Outputs:
- new_object: float32 [256, 2, 2, 128, 128], P('region')
The draws below stay inside these ranges and needn't reach their ends.
Inputs may be any that keep to these rules, and one draw needn't show every extreme that they name: A device's live positions are its first counts slots; the other slots of its position arrays are ignored. Some device holds 2 live positions. `row_offsets`: every slot of region index r starts at a row from r * 2 * 128 to r * 2 * 128 + 2 * 128 - 1, and never after row 3840.
All inputs are finite; a program needn't handle non-finite values.
Results may differ from the reference program's by a relative error of at most 0.0095.
Values sent between devices are 32-bit elements; how exact they have to be, the bound alone decides.
No kernel may reach another device: no remote copies, remote signals or barrier semaphores. Data moves between devices by JAX's collectives and lax.ppermute only.
A program may use at most 128 MiB of HBM per device.

```python
import math
import jax
import jax.numpy as jnp
from jax import lax

PIX = 256
MODES = 4
S = 2
TILE = 128
TGX = 8
BR = 2
POS_DEV = 2
NT = 256
TGY = 32
OH = 4096
OW = 1024
N_REGION = 16
N_POS = 8


def draw_counts(key, part):
    first_key, second_key = jax.random.split(key)
    heavy_rank = jax.random.randint(first_key, (N_REGION, N_POS), 0, 8) == 0
    chosen = jax.random.randint(second_key, (), 0, N_REGION * N_POS)
    places = jnp.arange(N_REGION * N_POS, dtype=jnp.int32).reshape(N_REGION, N_POS)
    return jnp.where(heavy_rank | (places == chosen), POS_DEV, 1).astype(jnp.int32)


def draw_row_offsets(key, part):
    band_rows = BR * TILE
    band_start = jnp.arange(N_REGION, dtype=jnp.int32)[:, None, None] * band_rows
    within = jax.random.randint(jax.random.fold_in(key, 11), (N_REGION, N_POS, POS_DEV), 0, band_rows)
    within = within.at[0, 0, 0].set(0)
    return jnp.minimum(band_start + within, OH - PIX).astype(jnp.int32)


def touch_ends(drawn, stream_key, low, largest):
    spot = [jax.random.randint(jax.random.fold_in(stream_key, axis), (), 0, length) for axis, length in enumerate(drawn.shape)]
    main_axis = drawn.shape.index(max(drawn.shape))
    beside = spot[:main_axis] + [(spot[main_axis] + 1) % drawn.shape[main_axis]] + spot[main_axis + 1:]
    return drawn.at[tuple(spot)].set(low).at[tuple(beside)].set(largest)


def level_of(own_key, dims, pieces, low, top_value):
    factor_of = 1.0
    for dim, shards_of in pieces:
        draws = jax.random.uniform(jax.random.fold_in(jax.random.fold_in(own_key, 6), dim), (shards_of,), jnp.float32, low / len(pieces), top_value / len(pieces))
        factor_of = factor_of * jnp.repeat(jnp.exp(draws), dims[dim] // shards_of).reshape((-1,) + (1,) * (len(dims) - 1 - dim))
    return factor_of


def scatter_about(key, extent, deviation, limit, cuts=(), kind=jnp.bfloat16):
    array = deviation * jax.random.normal(key, extent, jnp.float32)
    if cuts:
        array = array * level_of(key, extent, cuts, -0.22, 0.18)
    return jnp.clip(array, -limit, limit).astype(kind)


def setup_inputs(seed: int = 0) -> dict:
    key_of = jax.random.split(jax.random.key(seed), 8)
    object_tiles = scatter_about(key_of[0], (NT, S, 2, TILE, TILE), 0.7, 4.0, ((0, 16),), jnp.float32)
    probe = scatter_about(key_of[1], (MODES, 2, PIX, PIX), 0.5, 3.0, (), jnp.float32)
    fresnel_phase = jnp.clip(jax.random.uniform(key_of[2], (PIX, PIX), jnp.float32, -3.140625, 3.140625), -3.140625, 3.140625)
    patterns = jnp.clip(4.0 * jax.random.uniform(key_of[3], (N_REGION, N_POS, POS_DEV, PIX, PIX), jnp.float32) ** level_of(key_of[3], (N_REGION, N_POS, POS_DEV, PIX, PIX), ((0, 16), (1, 8)), -0.2, 0.2), 0.0, 4.0)
    row_offsets = draw_row_offsets(jax.random.fold_in(key_of[7], 71), 0)
    col_offsets = touch_ends(jax.random.randint(key_of[5], (N_REGION, N_POS, POS_DEV), 0, OW - PIX + 1), jax.random.fold_in(key_of[5], 1), 0, OW - PIX).astype(jnp.int32)
    counts = draw_counts(jax.random.fold_in(key_of[7], 71), 0)
    return dict(object_tiles=object_tiles, probe=probe, fresnel_phase=fresnel_phase, patterns=patterns, row_offsets=row_offsets, col_offsets=col_offsets, counts=counts)


step_size = 0.05

def make_tables(length):
    counter = jnp.arange(length, dtype=jnp.int32)
    product = counter[:, None] * counter[None, :] % length
    angles = product.astype(jnp.float32) * jnp.float32(2.0 * math.pi / length)
    factor = jnp.float32(1.0 / math.sqrt(length))
    return ((jnp.cos(angles) * factor).astype(jnp.bfloat16), (jnp.sin(angles) * factor).astype(jnp.bfloat16))

def left_product(matrix, field):
    return jnp.einsum('jk,mkl->mjl', matrix.astype(jnp.float32), field.astype(jnp.float32), precision=lax.Precision.HIGHEST)

def right_product(field, matrix):
    return jnp.einsum('mjk,kl->mjl', field.astype(jnp.float32), matrix.astype(jnp.float32), precision=lax.Precision.HIGHEST)

def transform(field_re, field_im, direction, cos_table, sin_table):
    field_re = field_re.astype(jnp.bfloat16)
    field_im = field_im.astype(jnp.bfloat16)
    upper_re = left_product(cos_table, field_re) - direction * left_product(sin_table, field_im)
    upper_im = left_product(cos_table, field_im) + direction * left_product(sin_table, field_re)
    upper_re = upper_re.astype(jnp.bfloat16)
    upper_im = upper_im.astype(jnp.bfloat16)
    result_re = right_product(upper_re, cos_table) - direction * right_product(upper_im, sin_table)
    result_im = right_product(upper_im, cos_table) + direction * right_product(upper_re, sin_table)
    return (result_re, result_im)

def complex_product(left_re, left_im, right_re, right_im):
    return (left_re * right_re - left_im * right_im, left_re * right_im + left_im * right_re)

def conj_product(left_re, left_im, right_re, right_im):
    return (left_re * right_re + left_im * right_im, left_re * right_im - left_im * right_re)

def position_gradient(patch, probe, wave_re, wave_im, measured, cos_table, sin_table):
    slice_count = patch.shape[0]
    field_re = probe[:, 0]
    field_im = probe[:, 1]
    incoming = []
    for layer_index in range(slice_count):
        incoming.append((field_re, field_im))
        exit_re, exit_im = complex_product(field_re, field_im, patch[layer_index, 0], patch[layer_index, 1])
        exit_re = exit_re.astype(jnp.bfloat16)
        exit_im = exit_im.astype(jnp.bfloat16)
        if layer_index + 1 < slice_count:
            spec_re, spec_im = transform(exit_re, exit_im, -1.0, cos_table, sin_table)
            spec_re, spec_im = complex_product(wave_re, wave_im, spec_re, spec_im)
            field_re, field_im = transform(spec_re.astype(jnp.bfloat16), spec_im.astype(jnp.bfloat16), 1.0, cos_table, sin_table)
    far_re, far_im = transform(exit_re, exit_im, -1.0, cos_table, sin_table)
    intensity = lax.optimization_barrier(jnp.sum(far_re * far_re + far_im * far_im, axis=0))
    misfit = intensity - measured
    back_re, back_im = transform((misfit * far_re).astype(jnp.bfloat16), (misfit * far_im).astype(jnp.bfloat16), 1.0, cos_table, sin_table)
    results = [None] * slice_count
    for layer_index in reversed(range(slice_count)):
        incident_re, incident_im = incoming[layer_index]
        grad_re, grad_im = conj_product(incident_re, incident_im, back_re, back_im)
        results[layer_index] = jnp.stack([lax.optimization_barrier(jnp.sum(grad_re, axis=0)), lax.optimization_barrier(jnp.sum(grad_im, axis=0))])
        if layer_index > 0:
            prior_re, prior_im = conj_product(patch[layer_index, 0], patch[layer_index, 1], back_re, back_im)
            spec_re, spec_im = transform(prior_re.astype(jnp.bfloat16), prior_im.astype(jnp.bfloat16), -1.0, cos_table, sin_table)
            spec_re, spec_im = conj_product(wave_re, wave_im, spec_re, spec_im)
            back_re, back_im = transform(spec_re.astype(jnp.bfloat16), spec_im.astype(jnp.bfloat16), 1.0, cos_table, sin_table)
    return jnp.stack(results)

def reference(object_tiles, probe, fresnel_phase, patterns, row_offsets, col_offsets, counts):
    image = object_tiles.reshape(TGY, TGX, S, 2, TILE, TILE).transpose(2, 3, 0, 4, 1, 5).reshape(S, 2, OH, OW)
    cos_table, sin_table = make_tables(PIX)
    wave_re = jnp.cos(fresnel_phase)
    wave_im = jnp.sin(fresnel_phase)
    measured = patterns.reshape(-1, PIX, PIX)
    row_start = row_offsets.reshape(-1).astype(jnp.int32)
    col_start = col_offsets.reshape(-1).astype(jnp.int32)
    slot_number = jnp.arange(POS_DEV, dtype=jnp.int32)
    alive = (slot_number[None, None, :] < counts[:, :, None]).reshape(-1)
    zero_index = jnp.int32(0)

    def visit(gradient, items):
        pattern, first_row, first_col, flag = items
        corner = (zero_index, zero_index, first_row, first_col)

        def compute(current):
            patch = lax.dynamic_slice(image, corner, (S, 2, PIX, PIX))
            term = position_gradient(patch, probe, wave_re, wave_im, pattern, cos_table, sin_table)
            former = lax.dynamic_slice(current, corner, (S, 2, PIX, PIX))
            return lax.dynamic_update_slice(current, former + term, corner)

        def unchanged(current):
            return current
        return (lax.cond(flag, compute, unchanged, gradient), None)
    gradient, _ = lax.scan(visit, jnp.zeros((S, 2, OH, OW), jnp.float32), (measured, row_start, col_start, alive))
    tile_gradient = gradient.reshape(S, 2, TGY, TILE, TGX, TILE).transpose(2, 4, 0, 1, 3, 5).reshape(NT, S, 2, TILE, TILE)
    return object_tiles - step_size * tile_gradient
```

```python
import functools
import math

import jax
import jax.numpy as jnp
import numpy as np
from jax import lax
from jax.experimental import pallas as pl
from jax.experimental.pallas import tpu as pltpu
from jax.sharding import PartitionSpec as P

STEP = 0.05
BOTH = ("region", "pos")
SUB = 8


def dft_blocks(length):
    counter = np.arange(length, dtype=np.int64)
    product = counter[:, None] * counter[None, :] % length
    angles = product.astype(np.float64) * (2.0 * math.pi / length)
    factor = 1.0 / math.sqrt(length)
    cos = np.cos(angles) * factor
    sin = np.sin(angles) * factor
    ahead = np.block([[cos, sin], [-sin, cos]]).astype(np.float32)
    behind = np.block([[cos, -sin], [sin, cos]]).astype(np.float32)
    return ahead.astype(jnp.bfloat16), behind.astype(jnp.bfloat16)


class Places:
    def __init__(self, mesh):
        self.regions = mesh.shape["region"]
        self.group = mesh.shape["pos"]
        self.ring = self.group // 2

    def flat(self, region, pos):
        return region * self.group + pos

    def turn(self, step, flip):
        pairs = []
        for region in range(self.regions):
            for pos in range(self.group):
                z, x = divmod(pos, self.ring)
                to = (z ^ flip) * self.ring + (x + step) % self.ring
                pairs.append((self.flat(region, pos), self.flat(region, to)))
        return pairs

    def upward(self):
        pairs = []
        for region in range(self.regions - 1):
            for pos in range(self.group):
                to = pos if region % 2 == 0 else (pos + self.ring) % self.group
                pairs.append((self.flat(region, pos), self.flat(region + 1, to)))
        return pairs

    def downward(self):
        return [(b, a) for a, b in self.upward()]

    def offsets(self):
        return [(step, flip) for flip in (0, 1) for step in range(self.ring)]


def send(value, pairs):
    return lax.ppermute(value, BOTH, pairs)


def full(memory_space=None):
    return pl.BlockSpec(memory_space=memory_space or pltpu.MemorySpace.VMEM)


SMEM = pltpu.MemorySpace.SMEM
VMEM = pltpu.MemorySpace.VMEM


def cut_window(tiles_ref, col, out_ref, across):
    tile = tiles_ref.shape[-1]
    downs = tiles_ref.shape[0] // across
    planes = tiles_ref.shape[1]
    first = col // tile
    shift = col - first * tile
    last = jnp.minimum(first + 2, across - 1)
    lane = lax.broadcasted_iota(jnp.int32, (tile, tile), 1)
    keep = lane < tile - shift
    back = (tile - shift) % tile
    for down in range(downs):
        for plane in range(planes):
            parts = []
            for index in (first, first + 1, last):
                value = tiles_ref[down * across + index, plane]
                parts.append(pltpu.roll(value, back, 1))
            rows = pl.ds(down * tile, tile)
            out_ref[plane, 0, rows, :] = jnp.where(keep, parts[0], parts[1])
            out_ref[plane, 1, rows, :] = jnp.where(keep, parts[1], parts[2])


def cut(tiles, cols, across):
    count, planes, tile, _ = tiles.shape
    rows = count // across * tile
    slots = cols.shape[0]

    def kernel(cols_ref, tiles_ref, *out_refs):
        for slot in range(slots):
            cut_window(tiles_ref, cols_ref[slot], out_refs[slot], across)

    return pl.pallas_call(
        kernel,
        out_shape=[jax.ShapeDtypeStruct((planes, 2, rows, tile), jnp.float32)] * slots,
        in_specs=[full(SMEM), full()],
        out_specs=[full()] * slots,
        name="cut",
    )(cols, tiles)


def own_class(tiles, klass, across):
    count, planes, tile, _ = tiles.shape
    downs = count // across
    per = tile // SUB

    def kernel(klass_ref, tiles_ref, out_ref):
        start = klass_ref[0]
        for down in range(downs):
            for over in range(across):
                for plane in range(planes):
                    out_ref[over, plane, pl.ds(down * per, per), :] = tiles_ref[
                        down * across + over, plane, pl.ds(start, per, stride=SUB), :
                    ]

    return pl.pallas_call(
        kernel,
        out_shape=jax.ShapeDtypeStruct((across, planes, downs * per, tile), jnp.float32),
        in_specs=[full(SMEM), full()],
        out_specs=full(),
        name="own_class",
    )(klass, tiles)


def position(meta, own, beyond, probe, wave, measured, ahead, behind, group, slot):
    modes = probe.shape[0]
    side = probe.shape[-1]
    planes = own.shape[0]
    tile = own.shape[-1]
    per = side // SUB
    bf16 = jnp.bfloat16

    def kernel(
        meta_ref, own_ref, beyond_ref, probe_ref, wave_ref, measured_ref, ahead_ref, behind_ref,
        *rest,
    ):
        out_refs = rest[:group]
        canvas_ref, patch_ref, inner_ref, far_ref, misfit_ref, grad_ref = rest[group : group + 6]
        left_ref, right_ref, sems = rest[group + 6 :]

        def matmul(a, b):
            return jnp.dot(a, b, preferred_element_type=jnp.float32)

        def transform(m, first_ref, second_ref):
            upper = matmul(first_ref[...], left_ref[m]).astype(bf16)
            right_ref[m, :, :side] = upper[:side]
            right_ref[m, :, side:] = upper[side:]
            both = matmul(right_ref[m], second_ref[...])
            return both[:, :side], both[:, side:]

        def put(m, re, im):
            left_ref[m, :side] = re.astype(bf16)
            left_ref[m, side:] = im.astype(bf16)

        def put_grad(m, plane, re, im):
            for index, value in ((plane, re), (plane + 1, im)):
                for half in range(2):
                    part = value[:, half * tile : (half + 1) * tile]
                    if m == 0:
                        grad_ref[index, half] = part
                    else:
                        grad_ref[index, half] += part

        def compute():
            copies = [
                pltpu.make_async_copy(own_ref, canvas_ref.at[:, :, pl.ds(0, side)], sems.at[0]),
                pltpu.make_async_copy(beyond_ref, canvas_ref.at[:, :, pl.ds(side, side)], sems.at[1]),
            ]
            for copy in copies:
                copy.start()
            for copy in copies:
                copy.wait()
            row = meta_ref[slot]
            for plane in range(planes):
                for half in range(2):
                    patch_ref[plane, :, pl.ds(half * tile, tile)] = canvas_ref[
                        plane, half, pl.ds(row, side), :
                    ]
            for m in range(modes):
                re, im = probe_ref[m, 0], probe_ref[m, 1]
                a, b = patch_ref[0], patch_ref[1]
                put(m, re * a - im * b, re * b + im * a)
            for m in range(modes):
                re, im = transform(m, ahead_ref, behind_ref)
                a, b = wave_ref[0], wave_ref[1]
                put(m, re * a - im * b, re * b + im * a)
            for m in range(modes):
                re, im = transform(m, behind_ref, ahead_ref)
                inner_ref[m, 0] = re
                inner_ref[m, 1] = im
                a, b = patch_ref[2], patch_ref[3]
                put(m, re * a - im * b, re * b + im * a)
            total = -measured_ref[slot]
            for m in range(modes):
                re, im = transform(m, ahead_ref, behind_ref)
                far_ref[m, 0] = re
                far_ref[m, 1] = im
                total = total + (re * re + im * im)
            misfit_ref[...] = total
            for m in range(modes):
                misfit = misfit_ref[...]
                put(m, misfit * far_ref[m, 0], misfit * far_ref[m, 1])
            for m in range(modes):
                re, im = transform(m, behind_ref, ahead_ref)
                a, b = inner_ref[m, 0], inner_ref[m, 1]
                term_re = a * re + b * im
                term_im = a * im - b * re
                put_grad(m, 2, term_re, term_im)
                a, b = patch_ref[2], patch_ref[3]
                put(m, a * re + b * im, a * im - b * re)
            for m in range(modes):
                re, im = transform(m, ahead_ref, behind_ref)
                a, b = wave_ref[0], wave_ref[1]
                put(m, a * re + b * im, a * im - b * re)
            for m in range(modes):
                re, im = transform(m, behind_ref, ahead_ref)
                a, b = probe_ref[m, 0], probe_ref[m, 1]
                term_re = a * re + b * im
                term_im = a * im - b * re
                put_grad(m, 0, term_re, term_im)
            for k in range(group):
                start = (meta_ref[8 + k] - row) & (SUB - 1)
                for plane in range(planes):
                    for half in range(2):
                        out_refs[k][plane, half] = grad_ref[
                            plane, half, pl.ds(start, per, stride=SUB), :
                        ]

        if slot == 0:
            compute()
        else:
            live = meta_ref[4] > slot
            pl.when(live)(compute)

            @pl.when(jnp.logical_not(live))
            def _():
                for k in range(group):
                    out_refs[k][...] = jnp.zeros_like(out_refs[k])

    any_space = pl.ANY
    return pl.pallas_call(
        kernel,
        out_shape=[jax.ShapeDtypeStruct((planes, 2, per, tile), jnp.float32)] * group,
        in_specs=[full(SMEM), full(any_space), full(any_space)] + [full()] * 5,
        out_specs=[full()] * group,
        scratch_shapes=[
            pltpu.VMEM((planes, 2, 2 * side, tile), jnp.float32),
            pltpu.VMEM((planes, side, side), jnp.float32),
            pltpu.VMEM((modes, 2, side, side), jnp.float32),
            pltpu.VMEM((modes, 2, side, side), jnp.float32),
            pltpu.VMEM((side, side), jnp.float32),
            pltpu.VMEM((planes, 2, side, tile), jnp.float32),
            pltpu.VMEM((modes, 2 * side, side), bf16),
            pltpu.VMEM((modes, side, 2 * side), bf16),
            pltpu.SemaphoreType.DMA((2,)),
        ],
        name="position",
    )(meta, own, beyond, probe, wave, measured, ahead, behind)


def gather_pieces(metas, klass, pieces, band_rows, across, tile, former, final):
    group = len(metas)
    slots = len(pieces)
    planes, _, per, _ = pieces[0][0].shape
    depth = 2 * band_rows // SUB
    slot_base = 0 if former is None else 1

    def kernel(*refs):
        klass_ref = refs[0]
        meta_refs = refs[1 : 1 + group]
        piece_refs = refs[1 + group : 1 + group + group]
        rest = refs[1 + 2 * group :]
        if former is not None:
            former_ref, rest = rest[0], rest[1:]
        if final:
            own_ref, spill_ref, sum_ref = rest
        else:
            (sum_ref,) = rest
        if former is None:
            sum_ref[...] = jnp.zeros_like(sum_ref)
        else:
            sum_ref[...] = former_ref[...]
        lane = lax.broadcasted_iota(jnp.int32, (per, tile), 1)
        k_class = klass_ref[0]
        for k in range(group):
            meta_ref = meta_refs[k]

            def add(meta_ref=meta_ref, piece_ref=piece_refs[k]):
                row = meta_ref[slot_base]
                col = meta_ref[2 + slot_base]
                start = (k_class - row) & (SUB - 1)
                down = (row + start - k_class) // SUB
                first = col // tile
                shift = col - first * tile
                keep = lane >= shift
                zero = jnp.zeros((per, tile), jnp.float32)
                for plane in range(planes):
                    left = pltpu.roll(piece_ref[plane, 0], shift, 1)
                    right = pltpu.roll(piece_ref[plane, 1], shift, 1)
                    rows = pl.ds(down, per)
                    sum_ref[first, plane, rows, :] += jnp.where(keep, left, zero)
                    sum_ref[first + 1, plane, rows, :] += jnp.where(keep, right, left)
                    sum_ref[first + 2, plane, rows, :] += jnp.where(keep, zero, right)

            if slot_base == 0:
                add()
            else:
                pl.when(meta_ref[4] > slot_base)(add)
        if final:
            for over in range(across):
                for plane in range(planes):
                    own_ref[over, plane] = sum_ref[over, plane, pl.ds(0, depth // 2), :]
                    spill_ref[over, plane] = sum_ref[over, plane, pl.ds(depth // 2, depth // 2), :]

    total = jax.ShapeDtypeStruct((across + 1, planes, depth, tile), jnp.float32)
    half = jax.ShapeDtypeStruct((across, planes, depth // 2, tile), jnp.float32)
    args = [klass, *metas, *pieces[0]]
    specs = [full(SMEM)] * (1 + group) + [full()] * group
    if former is not None:
        args.append(former)
        specs.append(full())
    return pl.pallas_call(
        kernel,
        out_shape=[half, half] if final else total,
        in_specs=specs,
        out_specs=[full(), full()] if final else full(),
        scratch_shapes=[pltpu.VMEM(total.shape, jnp.float32)] if final else [],
        name="sum_pieces",
    )(*args)


def update(held, own, arrived, slices):
    across, planes, rows, tile = held.shape
    each = planes // slices

    def kernel(held_ref, own_ref, arrived_ref, *out_refs):
        for s in range(slices):
            part = pl.ds(s * each, each)
            out_refs[s][...] = held_ref[:, part] - STEP * (own_ref[:, part] + arrived_ref[:, part])

    return pl.pallas_call(
        kernel,
        out_shape=[jax.ShapeDtypeStruct((across, each, rows, tile), jnp.float32)] * slices,
        in_specs=[full()] * 3,
        out_specs=[full()] * slices,
        name="update",
    )(held, own, arrived)


def assemble(order, shards, tiles_shape):
    count, planes, tile, _ = tiles_shape
    slices = len(shards)
    group = len(shards[0])
    flat_shards = [part for s in shards for k in s for part in k]
    shape = [[len(k) for k in s] for s in shards]
    per = tile // SUB

    def kernel(order_ref, *refs):
        out_ref = refs[-1]
        refs = list(refs[:-1])
        for s in range(slices):
            for k in range(group):
                start = order_ref[k]
                over = 0
                for _ in range(shape[s][k]):
                    ref = refs.pop(0)
                    across_part, each, rows, _ = ref.shape
                    downs = rows // per
                    across = count // downs
                    for o in range(across_part):
                        for down in range(downs):
                            for p in range(each):
                                out_ref[
                                    down * across + over + o, s * each + p,
                                    pl.ds(start, per, stride=SUB), :,
                                ] = ref[o, p, pl.ds(down * per, per), :]
                    over += across_part

    return pl.pallas_call(
        kernel,
        out_shape=jax.ShapeDtypeStruct(tiles_shape, jnp.float32),
        in_specs=[full(SMEM)] + [full()] * len(flat_shards),
        out_specs=full(),
        name="assemble",
    )(order, *flat_shards)


def around(shard, places):
    half = shard.shape[0] // 2
    up = send(shard, places.turn(1, 0))
    down = send(shard, places.turn(places.ring - 1, 0))
    far_a = send(up[:half], places.turn(1, 0))
    far_b = send(down[half:], places.turn(places.ring - 1, 0))
    return [[shard], [up], [far_a, far_b], [down]]


def per_device(
    places, object_tiles, probe, fresnel_phase, patterns, row_offsets, col_offsets, counts
):
    group = places.group
    ring = places.ring
    held_tiles, slices, _, tile, _ = object_tiles.shape
    slots = patterns.shape[2]
    side = patterns.shape[-1]
    across = TGX
    band_rows = held_tiles // across * tile
    tiles = object_tiles.reshape(held_tiles, slices * 2, tile, tile)
    region = lax.axis_index("region")
    pos = lax.axis_index("pos")
    measured = patterns.reshape(slots, side, side)
    rows = row_offsets.reshape(slots) - region * band_rows
    cols = col_offsets.reshape(slots)
    swap = (region // 2) % 2 * ring
    offsets = places.offsets()

    def class_of(step, flip, sign):
        z, x = pos // ring, pos % ring
        at = (z ^ flip) * ring + (x + sign * step) % ring
        return at ^ swap

    klass = class_of(0, 0, 1)
    to_class = [class_of(step, flip, 1) for step, flip in offsets]
    from_class = [class_of(step, flip, -1) for step, flip in offsets]
    meta = jnp.concatenate(
        [rows, cols, counts.reshape(1), jnp.zeros((3,), jnp.int32), jnp.stack(to_class)]
    ).astype(jnp.int32)
    klass1 = klass.reshape(1).astype(jnp.int32)
    order = jnp.stack(from_class).astype(jnp.int32)

    asked = send(cols, places.upward())
    lent = cut(tiles, asked, across)
    beyond = [send(window, places.downward()) for window in lent]
    own = cut(tiles, cols, across)
    held = own_class(tiles, klass1, across)
    wave = jnp.stack([jnp.cos(fresnel_phase), jnp.sin(fresnel_phase)])
    ahead, behind = (jnp.asarray(t) for t in dft_blocks(side))
    metas = [meta[:8]] + [send(meta[:8], places.turn(*o)) for o in offsets[1:]]

    def exchange(parts):
        return [parts[0]] + [
            send(part, places.turn(*o)) for part, o in zip(parts[1:], offsets[1:])
        ]

    total = None
    for slot in range(slots):
        parts = position(
            meta, own[slot], beyond[slot], probe, wave, measured, ahead, behind, group, slot
        )
        pieces = exchange(parts)
        total = gather_pieces(
            metas, klass1, [pieces], band_rows, across, tile, total, slot == slots - 1
        )
    own_sum, spill = total
    arrived = send(spill, places.upward())
    first, second = update(held, own_sum, arrived, slices)
    paired = send(first, places.turn(0, 1))
    shards_a = around(first, places) + around(paired, places)
    ringed = around(second, places)
    shards_b = ringed + [[send(p, places.turn(0, 1)) for p in k] for k in ringed]
    out = assemble(order, [shards_a, shards_b], tiles.shape)
    return out.reshape(object_tiles.shape)


TGX = 8


def solution(mesh):
    in_specs = (
        P("region", None, None, None, None),
        P(),
        P(),
        P("region", "pos", None, None, None),
        P("region", "pos", None),
        P("region", "pos", None),
        P("region", "pos"),
    )
    out_specs = P("region", None, None, None, None)
    return jax.shard_map(
        functools.partial(per_device, Places(mesh)),
        mesh=mesh, in_specs=in_specs, out_specs=out_specs, check_vma=False,
    )
```
